32 devices in a mesh: row: 4 (over y, core), col: 8 (over z, x).
Axes of the slice: x: 2, y: 2, z: 4, core: 2. Of those that a mesh axis runs over, the one named last changes fastest.
Arguments:
- positions: float32 [3, 16384], P(None, ('row', 'col')), may hold values from 0 to 4
- momenta: float32 [3, 16384], P(None, ('row', 'col')), may hold values from -6 to 6
- species: int32 [16384], P(('row', 'col')), may hold values from 0 to 1
- tile_a: int32 [4, 8, 256], P('row', 'col'), may hold values from 0 to 31, as said below
- tile_b: int32 [4, 8, 256], P('row', 'col'), may hold values from 0 to 15
- tile_count: int32 [4, 8], P('row', 'col'), may hold values from 1 to 256, as said below
Outputs:
- trial_positions: float32 [3, 16384], P(None, ('row', 'col'))
- trial_momenta: float32 [3, 16384], P(None, ('row', 'col'))
- end_force: float32 [3, 16384], P(None, ('row', 'col'))
The draws below stay inside these ranges and needn't reach their ends.
Inputs may be any that keep to these rules, and one draw needn't show every extreme that they name: Live slots of one grid cell name distinct (tile_a, tile_b) pairs; slots from tile_count on hold 0. `tile_count`: some grid cell of row 0 has exactly 256 live slots.
All inputs are finite; a program needn't handle non-finite values.
Results may differ from the reference program's by a relative error of at most 0.0003.
Values sent between devices are 32-bit elements; how exact they have to be, the bound alone decides.
A program may use at most 64 MiB of HBM per device.

```python
import jax
import jax.numpy as jnp
from jax import lax

TILE_DEV = 4
MAXP = 256
PARTICLES = 16384
N_ROW = 4
N_COL = 8


def pair_lists(key):
    key = jax.random.fold_in(key, 7)
    key_count, key_fill, key_perm = jax.random.split(key, 3)
    row_tiles = TILE_DEV * N_COL
    column_tiles = TILE_DEV * N_ROW
    rows = jnp.arange(N_ROW, dtype=jnp.int32)
    upper = MAXP * (1 + 3 * (N_ROW - 1 - rows)) // (1 + 3 * (N_ROW - 1))
    lower = jnp.maximum(upper // 2, 1)
    counts = jax.random.randint(key_count, (N_ROW, N_COL), lower[:, None], upper[:, None] + 1).astype(jnp.int32)
    filled = jax.random.randint(key_fill, (), 0, N_COL)
    counts = counts.at[0, filled].set(MAXP)
    device_keys = jax.random.split(key_perm, N_ROW * N_COL)
    orders = jax.vmap(lambda single: jax.random.permutation(single, row_tiles * column_tiles)[:MAXP])(device_keys)
    orders = orders.reshape(N_ROW, N_COL, MAXP).astype(jnp.int32)
    live = jnp.arange(MAXP, dtype=jnp.int32)[None, None, :] < counts[:, :, None]
    first = jnp.where(live, orders // column_tiles, 0).astype(jnp.int32)
    second = jnp.where(live, orders % column_tiles, 0).astype(jnp.int32)
    return (first, second, counts)


def draw_tile_a(key, part):
    return pair_lists(key)[0]


def draw_tile_b(key, part):
    return pair_lists(key)[1]


def draw_tile_count(key, part):
    return pair_lists(key)[2]


def set_ends(array, stream_key, smallest, largest):
    extent = array.shape
    spot = [jax.random.randint(jax.random.fold_in(stream_key, axis), (), 0, extent[axis]) for axis in range(len(extent))]
    array = array.at[tuple(spot)].set(smallest)
    longest = extent.index(max(extent))
    spot[longest] = (spot[longest] + 1) % extent[longest]
    return array.at[tuple(spot)].set(largest)


def block_scale(rng, dims, pieces, low, top_value):
    factor_of, own = 1.0, jax.random.fold_in(rng, 6)
    for position, shards_of in pieces:
        draws = jnp.exp(jax.random.uniform(jax.random.fold_in(own, position), (shards_of,), jnp.float32, low / len(pieces), top_value / len(pieces)))
        factor_of = factor_of * jnp.repeat(draws, dims[position] // shards_of).reshape([-1 if axis == position else 1 for axis in range(len(dims))])
    return factor_of


def normal_values(key, extent, spread, limit, cuts=(), kind=jnp.bfloat16):
    loudness = block_scale(key, extent, cuts, -0.22, 0.18) if cuts else 1.0
    entries = jax.random.normal(key, extent, jnp.float32) * spread * loudness
    return jnp.minimum(jnp.maximum(entries, -limit), limit).astype(kind)


def setup_inputs(seed: int = 0) -> dict:
    keys = jax.random.split(jax.random.key(seed), 7)
    positions = jnp.clip(4.0 * jax.random.uniform(keys[0], (3, PARTICLES), jnp.float32) ** block_scale(keys[0], (3, PARTICLES), ((1, 32),), -0.2, 0.2), 0.0, 4.0)
    momenta = normal_values(keys[1], (3, PARTICLES), 1.0, 6.0, ((1, 32),), jnp.float32)
    species = set_ends(jax.random.randint(keys[2], (PARTICLES,), 0, 2), jax.random.fold_in(keys[2], 1), 0, 1).astype(jnp.int32)
    tile_a = draw_tile_a(jax.random.fold_in(keys[6], 71), 0)
    tile_b = draw_tile_b(jax.random.fold_in(keys[6], 71), 0)
    tile_count = draw_tile_count(jax.random.fold_in(keys[6], 71), 0)
    return dict(positions=positions, momenta=momenta, species=species, tile_a=tile_a, tile_b=tile_b, tile_count=tile_count)


SCREENING = 1.0
SOFTENING = 0.25
GRAVITY = 0.5
LIGHT_CHARGE = 1.0
HEAVY_CHARGE = 2.5
HALF_STEP = 0.1
TIME_STEP = 0.2
tile_width = 128

def tile_pair_force(near, far, same):
    offset = near[:3, :, :, None] - far[:3, :, None, :]
    radius = jnp.sqrt(lax.optimization_barrier(jnp.sum(offset * offset, axis=0)) + SOFTENING)
    weight = near[3][:, :, None] * far[3][:, None, :] * jnp.exp(-SCREENING * radius) * (1.0 + SCREENING * radius) / (radius * radius * radius)
    diagonal = jnp.arange(tile_width)[:, None] == jnp.arange(tile_width)[None, :]
    weight = jnp.where(jnp.logical_and(same[:, None, None], diagonal[None]), 0.0, weight)
    return jnp.transpose(lax.optimization_barrier(jnp.sum(weight[None] * offset, axis=3)), (1, 0, 2))

def weight_of(mass):
    return jnp.zeros((3, mass.shape[0]), jnp.float32).at[2].set(-GRAVITY * mass)

def reference(positions, momenta, species, tile_a, tile_b, tile_count):
    charge = jnp.where(species == 1, HEAVY_CHARGE, LIGHT_CHARGE).astype(jnp.float32)
    total_tiles = positions.shape[1] // tile_width
    row_ids = jnp.arange(N_ROW, dtype=jnp.int32)[:, None, None]
    col_ids = jnp.arange(N_COL, dtype=jnp.int32)[None, :, None]
    firsts = (row_ids * N_COL * TILE_DEV + tile_a).astype(jnp.int32).reshape(-1, MAXP)
    seconds = ((tile_b // TILE_DEV * N_COL + col_ids) * TILE_DEV + tile_b % TILE_DEV).astype(jnp.int32).reshape(-1, MAXP)
    live = (jnp.arange(MAXP, dtype=jnp.int32)[None, None, :] < tile_count[:, :, None]).reshape(-1, MAXP)
    gravity = weight_of(charge)

    def forces(places):
        state = jnp.concatenate([places, charge[None]], axis=0).reshape(4, total_tiles, tile_width)

        def visit(total, block):
            first, second, alive = block
            term = tile_pair_force(state[:, first], state[:, second], first == second)
            term = term * alive.astype(jnp.float32)[:, None, None]
            return (total.at[first].add(term), None)
        total, _ = lax.scan(visit, jnp.zeros((total_tiles, 3, tile_width), jnp.float32), (firsts, seconds, live))
        return jnp.transpose(total, (1, 0, 2)).reshape(3, -1) + gravity
    start_force = forces(positions)
    half = momenta + HALF_STEP * start_force
    moved = positions + TIME_STEP * half / charge
    end_force = forces(moved)
    ahead = half + HALF_STEP * end_force
    return (moved, ahead, end_force)
```

```python
import functools
import math

import jax
import jax.numpy as jnp
from jax import lax
from jax.experimental import pallas as pl
from jax.experimental.pallas import tpu as pltpu
from jax.sharding import PartitionSpec as P

SOFTENING = 0.25
GRAVITY = 0.5
LIGHT_CHARGE = 1.0
HEAVY_CHARGE = 2.5
HALF_STEP = 0.1
TIME_STEP = 0.2
tile_width = 128
unroll = 4
scale = 1.0 / math.log(2.0)
middle = 2.0
depth = 32
MESH = pl.DeviceIdType.MESH


def peers_of(axes):
    found = []
    for axis, size in axes:
        me = lax.axis_index(axis)
        for step in range(1, size):
            found.append((axis, lax.rem(me + step, size)))
    return found


def greet(axes):
    barrier = pltpu.get_barrier_semaphore()
    everyone = peers_of(axes)
    for axis, peer in everyone:
        pl.semaphore_signal(barrier, inc=1, device_id={axis: peer}, device_id_type=MESH)
    pl.semaphore_wait(barrier, len(everyone))


def charge_of(species):
    return jnp.where(species == 1, HEAVY_CHARGE, LIGHT_CHARGE).astype(jnp.float32)


def spread(axes, packed, slots, send_sem, recv_sem):
    copies = []
    for (axis, size), buffer in zip(axes, slots):
        me = lax.axis_index(axis)
        for step in range(1, size):
            which = len(copies)
            copies.append(
                pltpu.make_async_remote_copy(
                    src_ref=packed,
                    dst_ref=buffer.at[me],
                    send_sem=send_sem.at[which],
                    recv_sem=recv_sem.at[which],
                    device_id={axis: lax.rem(me + step, size)},
                    device_id_type=MESH,
                )
            )
    for copy in copies:
        copy.start()
    for (axis, size), buffer in zip(axes, slots):
        buffer[pl.ds(lax.axis_index(axis), 1)] = packed[...][None]
    for copy in copies:
        copy.wait()


def pack(packed, places, charge, tiles):
    for tile in range(tiles):
        lanes = slice(tile * tile_width, (tile + 1) * tile_width)
        packed[4 * tile : 4 * tile + 3, :] = places[:, lanes]
        packed[4 * tile + 3 : 4 * tile + 4, :] = charge[:, lanes]


def gather_kernel(axes, tiles, pos_ref, spec_ref, rows_ref, cols_ref, packed, send_sem, recv_sem):
    greet(axes)
    pack(packed, pos_ref[...], charge_of(spec_ref[...]), tiles)
    spread(axes, packed, (rows_ref, cols_ref), send_sem, recv_sem)


def collect(axis, size, partial, arrived, send_sem, recv_sem):
    me = lax.axis_index(axis)
    copies = []
    for step in range(1, size):
        peer = lax.rem(me + step, size)
        copies.append(
            pltpu.make_async_remote_copy(
                src_ref=partial.at[peer],
                dst_ref=arrived.at[me],
                send_sem=send_sem.at[step - 1],
                recv_sem=recv_sem.at[step - 1],
                device_id={axis: peer},
                device_id_type=MESH,
            )
        )
    for copy in copies:
        copy.start()
    arrived[pl.ds(me, 1)] = partial[pl.ds(me, 1)]
    for copy in copies:
        copy.wait()
    total = arrived[0]
    for index in range(1, size):
        total = total + arrived[index]
    return total


def unpacked(total, charge, tiles):
    force = jnp.concatenate([total[4 * tile : 4 * tile + 3, :] for tile in range(tiles)], axis=1)
    third = lax.broadcasted_iota(jnp.int32, force.shape, 0) == 2
    return force + jnp.where(third, -GRAVITY * charge, 0.0)


def step_kernel(
    axes, tiles, part_ref, pos_ref, mom_ref, spec_ref, rows_ref, cols_ref, moved_ref, half_ref,
    arrived, packed, send_a, recv_a, send_b, recv_b,
):
    greet(axes)
    charge = charge_of(spec_ref[...])
    total = collect(axes[0][0], axes[0][1], part_ref, arrived, send_a, recv_a)
    force = unpacked(total, charge, tiles)
    half = mom_ref[...] + HALF_STEP * force
    moved = pos_ref[...] + TIME_STEP * half / charge
    half_ref[...] = half
    moved_ref[...] = moved
    pack(packed, moved, charge, tiles)
    spread(axes, packed, (rows_ref, cols_ref), send_b, recv_b)


def last_kernel(axes, tiles, part_ref, half_ref, spec_ref, ahead_ref, force_ref, arrived, send_a, recv_a):
    greet(axes)
    charge = charge_of(spec_ref[...])
    total = collect(axes[0][0], axes[0][1], part_ref, arrived, send_a, recv_a)
    force = unpacked(total, charge, tiles)
    force_ref[...] = force
    ahead_ref[...] = half_ref[...] + HALF_STEP * force


def pieces(value):
    high = value.astype(jnp.bfloat16).astype(jnp.float32)
    rest = value - high
    mid = rest.astype(jnp.bfloat16).astype(jnp.float32)
    return high, mid, (rest - mid).astype(jnp.bfloat16).astype(jnp.float32)


pairs_of_pieces = ((0, 0), (0, 1), (1, 0), (0, 2), (2, 0), (1, 1))


def force_kernel(
    tiles, first_ref, second_ref, count_ref, rows_ref, cols_ref, out_ref,
    near_f, near, far_f, far, load_f, load, total,
):
    near_f[...] = jnp.zeros_like(near_f)
    far_f[...] = jnp.zeros_like(far_f)
    load_f[...] = jnp.zeros_like(load_f)
    total[...] = jnp.zeros_like(total)

    def component(ref, owner, index):
        return ref[owner, pl.ds(index, tiles, stride=4), :]

    for owner in range(rows_ref.shape[0]):
        here = pl.ds(owner * tiles, tiles)
        square = 0.0
        for axis in range(3):
            value = (component(rows_ref, owner, axis) - middle) * scale
            square = square + value * value
            split = pieces(value)
            for row, (left, _) in enumerate(pairs_of_pieces):
                near_f[here, 6 * axis + row, :] = -2.0 * split[left]
        for row, piece in enumerate(pieces(square)):
            near_f[here, 18 + row, :] = piece
            near_f[here, 21 + row, :] = jnp.ones_like(piece)
    near[...] = near_f[...].astype(jnp.bfloat16)

    for owner in range(cols_ref.shape[0]):
        here = pl.ds(owner * tiles, tiles)
        charge = component(cols_ref, owner, 3)
        square = SOFTENING * scale * scale
        for axis in range(3):
            value = (component(cols_ref, owner, axis) - middle) * scale
            square = square + value * value
            split = pieces(value)
            for row, (_, right) in enumerate(pairs_of_pieces):
                far_f[here, 6 * axis + row, :] = split[right]
            for row, piece in enumerate(pieces(charge * value)):
                load_f[here, 4 * row + axis, :] = piece
        load_f[here, 3, :] = charge
        for row, piece in enumerate(pieces(square)):
            far_f[here, 18 + row, :] = jnp.ones_like(piece)
            far_f[here, 21 + row, :] = piece
    for tile in range(cols_ref.shape[0] * tiles):
        far[tile] = far_f[tile].T.astype(jnp.bfloat16)
    single = load_f[...].astype(jnp.bfloat16)
    load[:, :, :tile_width] = single
    load[:, :, tile_width:] = single

    count = count_ref[0]

    def visit(step, carry):
        start = step * unroll
        firsts = [first_ref[start + index] for index in range(unroll)]
        seconds = [second_ref[start + index] for index in range(unroll)]
        terms = []
        for index in range(unroll):
            square = jnp.dot(far[seconds[index]], near[firsts[index]], preferred_element_type=jnp.float32)
            square = jnp.maximum(square, SOFTENING * scale * scale)
            inverse = lax.rsqrt(square)
            decay = jnp.exp2(-(square * inverse))
            weight = decay * (inverse * inverse) * (inverse + 1.0 / scale)
            high = weight.astype(jnp.bfloat16)
            low = (weight - high.astype(jnp.float32)).astype(jnp.bfloat16)
            both = jnp.concatenate([high, low], axis=0)
            term = jnp.dot(load[seconds[index]], both, preferred_element_type=jnp.float32)
            terms.append(jnp.where(start + index < count, term, 0.0))
        for index in range(unroll):
            total[firsts[index]] += terms[index]
        return carry

    lax.fori_loop(0, (count + unroll - 1) // unroll, visit, 0)

    for owner in range(rows_ref.shape[0]):
        here = pl.ds(owner * tiles, tiles)
        charge = component(rows_ref, owner, 3) * (scale * scale)
        weights = total[here, 3, :]
        for axis in range(3):
            value = (component(rows_ref, owner, axis) - middle) * scale
            moment = total[here, axis, :] + total[here, 4 + axis, :] + total[here, 8 + axis, :]
            out_ref[owner, pl.ds(axis, tiles, stride=4), :] = charge * (value * weights - moment)
        out_ref[owner, pl.ds(3, tiles, stride=4), :] = jnp.zeros_like(charge)


def per_device(row_count, col_count, positions, momenta, species, tile_a, tile_b, tile_count):
    own = positions.shape[1]
    tiles = own // tile_width
    f32 = jnp.float32
    axes = (("col", col_count), ("row", row_count))
    others = row_count + col_count - 2
    vmem = pl.BlockSpec(memory_space=pltpu.VMEM)
    smem = pl.BlockSpec(memory_space=pltpu.SMEM)
    labels = species.reshape(1, own)
    slots = tile_a.shape[-1]
    padding = -slots % unroll
    firsts = jnp.pad(tile_a.reshape(slots), (0, padding))
    seconds = jnp.pad(tile_b.reshape(slots), (0, padding))
    count = tile_count.reshape(1)
    row_shape = jax.ShapeDtypeStruct((col_count, 4 * tiles, tile_width), f32)
    col_shape = jax.ShapeDtypeStruct((row_count, 4 * tiles, tile_width), f32)
    own_shape = jax.ShapeDtypeStruct((3, own), f32)
    DMA = pltpu.SemaphoreType.DMA

    rows, cols = pl.pallas_call(
        functools.partial(gather_kernel, axes, tiles),
        out_shape=(row_shape, col_shape),
        in_specs=[vmem] * 2,
        out_specs=(vmem, vmem),
        scratch_shapes=[pltpu.VMEM((4 * tiles, tile_width), f32), DMA((others,)), DMA((others,))],
        compiler_params=pltpu.CompilerParams(collective_id=0, has_side_effects=True),
        name="gather",
    )(positions, labels)

    near_count, far_count = col_count * tiles, row_count * tiles
    bf16 = jnp.bfloat16
    forces = pl.pallas_call(
        functools.partial(force_kernel, tiles),
        out_shape=row_shape,
        in_specs=[smem] * 3 + [vmem] * 2,
        out_specs=vmem,
        scratch_shapes=[
            pltpu.VMEM((near_count, depth, tile_width), f32),
            pltpu.VMEM((near_count, depth, tile_width), bf16),
            pltpu.VMEM((far_count, depth, tile_width), f32),
            pltpu.VMEM((far_count, tile_width, depth), bf16),
            pltpu.VMEM((far_count, 16, tile_width), f32),
            pltpu.VMEM((far_count, 16, 2 * tile_width), bf16),
            pltpu.VMEM((near_count, 16, tile_width), f32),
        ],
        compiler_params=pltpu.CompilerParams(vmem_limit_bytes=32 << 20),
        name="forces",
    )

    partial = forces(firsts, seconds, count, rows, cols)
    rows, cols, moved, half = pl.pallas_call(
        functools.partial(step_kernel, axes, tiles),
        out_shape=(row_shape, col_shape, own_shape, own_shape),
        in_specs=[vmem] * 4,
        out_specs=(vmem,) * 4,
        scratch_shapes=[
            pltpu.VMEM(row_shape.shape, f32),
            pltpu.VMEM((4 * tiles, tile_width), f32),
            DMA((col_count - 1,)),
            DMA((col_count - 1,)),
            DMA((others,)),
            DMA((others,)),
        ],
        compiler_params=pltpu.CompilerParams(collective_id=1, has_side_effects=True),
        name="step",
    )(partial, positions, momenta, labels)

    partial = forces(firsts, seconds, count, rows, cols)
    ahead, end_force = pl.pallas_call(
        functools.partial(last_kernel, axes[:1], tiles),
        out_shape=(own_shape, own_shape),
        in_specs=[vmem] * 3,
        out_specs=(vmem,) * 2,
        scratch_shapes=[pltpu.VMEM(row_shape.shape, f32), DMA((col_count - 1,)), DMA((col_count - 1,))],
        compiler_params=pltpu.CompilerParams(collective_id=2, has_side_effects=True),
        name="last",
    )(partial, half, labels)
    return (moved, ahead, end_force)


def solution(mesh):
    in_specs = (
        P(None, ("row", "col")),
        P(None, ("row", "col")),
        P(("row", "col")),
        P("row", "col", None),
        P("row", "col", None),
        P("row", "col"),
    )
    out_specs = (P(None, ("row", "col")), P(None, ("row", "col")), P(None, ("row", "col")))
    body = functools.partial(per_device, mesh.shape["row"], mesh.shape["col"])
    return jax.shard_map(body, mesh=mesh, in_specs=in_specs, out_specs=out_specs, check_vma=False)
```

```python
import functools
import math

import jax
import jax.numpy as jnp
from jax import lax
from jax.experimental import pallas as pl
from jax.experimental.pallas import tpu as pltpu
from jax.sharding import PartitionSpec as P

SOFTENING = 0.25
GRAVITY = 0.5
LIGHT_CHARGE = 1.0
HEAVY_CHARGE = 2.5
HALF_STEP = 0.1
TIME_STEP = 0.2
tile_width = 128
unroll = 32
scale = 1.0 / math.log(2.0)
middle = 2.0
depth = 32
MESH = pl.DeviceIdType.MESH


def peers_of(axes):
    found = []
    for axis, size in axes:
        me = lax.axis_index(axis)
        for step in range(1, size):
            found.append((axis, lax.rem(me + step, size)))
    return found


def greet(axes):
    barrier = pltpu.get_barrier_semaphore()
    everyone = peers_of(axes)
    for axis, peer in everyone:
        pl.semaphore_signal(barrier, inc=1, device_id={axis: peer}, device_id_type=MESH)
    pl.semaphore_wait(barrier, len(everyone))


def charge_of(species):
    return jnp.where(species == 1, HEAVY_CHARGE, LIGHT_CHARGE).astype(jnp.float32)


def spread(axes, packed, slots, send_sem, recv_sem, own_sem):
    copies = []
    for (axis, size), buffer in zip(axes, slots):
        me = lax.axis_index(axis)
        for step in range(1, size):
            which = len(copies)
            copies.append(
                pltpu.make_async_remote_copy(
                    src_ref=packed,
                    dst_ref=buffer.at[me],
                    send_sem=send_sem.at[which],
                    recv_sem=recv_sem.at[which],
                    device_id={axis: lax.rem(me + step, size)},
                    device_id_type=MESH,
                )
            )
    for copy in copies:
        copy.start()
    kept = [
        pltpu.make_async_copy(packed, buffer.at[lax.axis_index(axis)], own_sem.at[index])
        for index, ((axis, size), buffer) in enumerate(zip(axes, slots))
    ]
    for copy in kept:
        copy.start()
    for copy in kept + copies:
        copy.wait()


def pack(packed, places, charge, tiles):
    for tile in range(tiles):
        lanes = slice(tile * tile_width, (tile + 1) * tile_width)
        packed[4 * tile : 4 * tile + 3, :] = places[:, lanes]
        packed[4 * tile + 3 : 4 * tile + 4, :] = charge[:, lanes]


def gather_kernel(axes, tiles, pos_ref, spec_ref, rows_ref, cols_ref, packed, send_sem, recv_sem, own_sem):
    greet(axes)
    pack(packed, pos_ref[...], charge_of(spec_ref[...]), tiles)
    spread(axes, packed, (rows_ref, cols_ref), send_sem, recv_sem, own_sem)


def collect(axis, size, partial, arrived, send_sem, recv_sem, own_sem):
    me = lax.axis_index(axis)
    copies = []
    for step in range(1, size):
        peer = lax.rem(me + step, size)
        copies.append(
            pltpu.make_async_remote_copy(
                src_ref=partial.at[peer],
                dst_ref=arrived.at[me],
                send_sem=send_sem.at[step - 1],
                recv_sem=recv_sem.at[step - 1],
                device_id={axis: peer},
                device_id_type=MESH,
            )
        )
    for copy in copies:
        copy.start()
    kept = pltpu.make_async_copy(partial.at[me], arrived.at[me], own_sem.at[0])
    kept.start()
    for copy in [kept] + copies:
        copy.wait()
    total = arrived[0]
    for index in range(1, size):
        total = total + arrived[index]
    return total


def unpacked(total, charge, tiles):
    force = jnp.concatenate([total[4 * tile : 4 * tile + 3, :] for tile in range(tiles)], axis=1)
    third = lax.broadcasted_iota(jnp.int32, force.shape, 0) == 2
    return force + jnp.where(third, -GRAVITY * charge, 0.0)


def step_kernel(
    axes, tiles, part_ref, pos_ref, mom_ref, spec_ref, rows_ref, cols_ref, moved_ref, half_ref,
    arrived, packed, send_a, recv_a, send_b, recv_b, own_sem,
):
    greet(axes)
    charge = charge_of(spec_ref[...])
    total = collect(axes[0][0], axes[0][1], part_ref, arrived, send_a, recv_a, own_sem)
    force = unpacked(total, charge, tiles)
    half = mom_ref[...] + HALF_STEP * force
    moved = pos_ref[...] + TIME_STEP * half / charge
    half_ref[...] = half
    moved_ref[...] = moved
    pack(packed, moved, charge, tiles)
    spread(axes, packed, (rows_ref, cols_ref), send_b, recv_b, own_sem.at[pl.ds(1, 2)])


def last_kernel(axes, tiles, part_ref, spec_ref, force_ref, arrived, send_a, recv_a, own_sem):
    greet(axes)
    charge = charge_of(spec_ref[...])
    total = collect(axes[0][0], axes[0][1], part_ref, arrived, send_a, recv_a, own_sem)
    force_ref[...] = unpacked(total, charge, tiles)


def finish_kernel(moved_ref, half_ref, force_ref, trial_ref, ahead_ref, end_ref):
    trial_ref[...] = moved_ref[...]
    ahead_ref[...] = half_ref[...] + HALF_STEP * force_ref[...]
    end_ref[...] = force_ref[...]


def pieces(value):
    high = value.astype(jnp.bfloat16).astype(jnp.float32)
    rest = value - high
    mid = rest.astype(jnp.bfloat16).astype(jnp.float32)
    return high, mid, (rest - mid).astype(jnp.bfloat16).astype(jnp.float32)


pairs_of_pieces = ((0, 0), (0, 1), (1, 0), (0, 2), (2, 0), (1, 1))


def force_kernel(
    tiles, first_ref, second_ref, count_ref, rows_hbm, cols_hbm, out_hbm,
    out_ref, rows_ref, cols_ref, near_f, near, far_f, far, load_f, load, total, sems,
):
    fetches = [
        pltpu.make_async_copy(rows_hbm, rows_ref, sems.at[0]),
        pltpu.make_async_copy(cols_hbm, cols_ref, sems.at[1]),
    ]
    for fetch in fetches:
        fetch.start()
    near_f[...] = jnp.zeros_like(near_f)
    far_f[...] = jnp.zeros_like(far_f)
    load_f[...] = jnp.zeros_like(load_f)
    total[...] = jnp.zeros_like(total)
    for fetch in fetches:
        fetch.wait()

    def component(ref, owner, index):
        return ref[owner, pl.ds(index, tiles, stride=4), :]

    for owner in range(rows_ref.shape[0]):
        here = pl.ds(owner * tiles, tiles)
        square = 0.0
        for axis in range(3):
            value = (component(rows_ref, owner, axis) - middle) * scale
            square = square + value * value
            split = pieces(value)
            for row, (left, _) in enumerate(pairs_of_pieces):
                near_f[here, 6 * axis + row, :] = -2.0 * split[left]
        for row, piece in enumerate(pieces(square)):
            near_f[here, 18 + row, :] = piece
            near_f[here, 21 + row, :] = jnp.ones_like(piece)
    near[...] = near_f[...].astype(jnp.bfloat16)

    for owner in range(cols_ref.shape[0]):
        here = pl.ds(owner * tiles, tiles)
        charge = component(cols_ref, owner, 3)
        square = SOFTENING * scale * scale
        for axis in range(3):
            value = (component(cols_ref, owner, axis) - middle) * scale
            square = square + value * value
            split = pieces(value)
            for row, (_, right) in enumerate(pairs_of_pieces):
                far_f[here, 6 * axis + row, :] = split[right]
            for row, piece in enumerate(pieces(charge * value)):
                load_f[here, 4 * row + axis, :] = piece
        load_f[here, 3, :] = charge
        for row, piece in enumerate(pieces(square)):
            far_f[here, 18 + row, :] = jnp.ones_like(piece)
            far_f[here, 21 + row, :] = piece
    for tile in range(cols_ref.shape[0] * tiles):
        far[tile] = far_f[tile].T.astype(jnp.bfloat16)
    single = load_f[...].astype(jnp.bfloat16)
    load[:, :, :tile_width] = single
    load[:, :, tile_width:] = single

    count = count_ref[0]

    def visit(step, carry):
        start = step * unroll
        firsts = [first_ref[start + index] for index in range(unroll)]
        seconds = [second_ref[start + index] for index in range(unroll)]
        terms = []
        for index in range(unroll):
            square = jnp.dot(far[seconds[index]], near[firsts[index]], preferred_element_type=jnp.float32)
            square = jnp.maximum(square, SOFTENING * scale * scale)
            inverse = lax.rsqrt(square)
            decay = jnp.exp2(-(square * inverse))
            weight = decay * (inverse * inverse) * (inverse + 1.0 / scale)
            high = weight.astype(jnp.bfloat16)
            low = (weight - high.astype(jnp.float32)).astype(jnp.bfloat16)
            both = jnp.concatenate([high, low], axis=0)
            term = jnp.dot(load[seconds[index]], both, preferred_element_type=jnp.float32)
            terms.append(jnp.where(start + index < count, term, 0.0))
        for index in range(unroll):
            total[firsts[index]] += terms[index]
        return carry

    lax.fori_loop(0, (count + unroll - 1) // unroll, visit, 0)

    for owner in range(rows_ref.shape[0]):
        here = pl.ds(owner * tiles, tiles)
        charge = component(rows_ref, owner, 3) * (scale * scale)
        weights = total[here, 3, :]
        for axis in range(3):
            value = (component(rows_ref, owner, axis) - middle) * scale
            moment = total[here, axis, :] + total[here, 4 + axis, :] + total[here, 8 + axis, :]
            out_ref[owner, pl.ds(axis, tiles, stride=4), :] = charge * (value * weights - moment)
        out_ref[owner, pl.ds(3, tiles, stride=4), :] = jnp.zeros_like(charge)
    pltpu.sync_copy(out_ref, out_hbm)


def per_device(row_count, col_count, positions, momenta, species, tile_a, tile_b, tile_count):
    own = positions.shape[1]
    tiles = own // tile_width
    f32 = jnp.float32
    axes = (("col", col_count), ("row", row_count))
    others = row_count + col_count - 2
    vmem = pl.BlockSpec(memory_space=pltpu.VMEM)
    anywhere = pl.BlockSpec(memory_space=pltpu.HBM)
    smem = pl.BlockSpec(memory_space=pltpu.SMEM)
    labels = species.reshape(1, own)
    slots = tile_a.shape[-1]
    padding = -slots % unroll
    firsts = jnp.pad(tile_a.reshape(slots), (0, padding))
    seconds = jnp.pad(tile_b.reshape(slots), (0, padding))
    count = tile_count.reshape(1)
    row_shape = jax.ShapeDtypeStruct((col_count, 4 * tiles, tile_width), f32)
    col_shape = jax.ShapeDtypeStruct((row_count, 4 * tiles, tile_width), f32)
    own_shape = jax.ShapeDtypeStruct((3, own), f32)
    DMA = pltpu.SemaphoreType.DMA

    rows, cols = pl.pallas_call(
        functools.partial(gather_kernel, axes, tiles),
        out_shape=(row_shape, col_shape),
        in_specs=[vmem] * 2,
        out_specs=(anywhere, anywhere),
        scratch_shapes=[
            pltpu.VMEM((4 * tiles, tile_width), f32), DMA((others,)), DMA((others,)), DMA((2,)),
        ],
        compiler_params=pltpu.CompilerParams(collective_id=0, has_side_effects=True),
        name="gather",
    )(positions, labels)

    near_count, far_count = col_count * tiles, row_count * tiles
    bf16 = jnp.bfloat16
    forces = pl.pallas_call(
        functools.partial(force_kernel, tiles),
        out_shape=row_shape,
        in_specs=[smem] * 3 + [anywhere] * 2,
        out_specs=anywhere,
        scratch_shapes=[
            pltpu.VMEM(row_shape.shape, f32),
            pltpu.VMEM(row_shape.shape, f32),
            pltpu.VMEM(col_shape.shape, f32),
            pltpu.VMEM((near_count, depth, tile_width), f32),
            pltpu.VMEM((near_count, depth, tile_width), bf16),
            pltpu.VMEM((far_count, depth, tile_width), f32),
            pltpu.VMEM((far_count, tile_width, depth), bf16),
            pltpu.VMEM((far_count, 16, tile_width), f32),
            pltpu.VMEM((far_count, 16, 2 * tile_width), bf16),
            pltpu.VMEM((near_count, 16, tile_width), f32),
            DMA((2,)),
        ],
        name="forces",
    )

    partial = forces(firsts, seconds, count, rows, cols)
    rows, cols, moved, half = pl.pallas_call(
        functools.partial(step_kernel, axes, tiles),
        out_shape=(row_shape, col_shape, own_shape, own_shape),
        in_specs=[anywhere] + [vmem] * 3,
        out_specs=(anywhere, anywhere, vmem, vmem),
        scratch_shapes=[
            pltpu.VMEM(row_shape.shape, f32),
            pltpu.VMEM((4 * tiles, tile_width), f32),
            DMA((col_count - 1,)),
            DMA((col_count - 1,)),
            DMA((others,)),
            DMA((others,)),
            DMA((3,)),
        ],
        compiler_params=pltpu.CompilerParams(collective_id=1, has_side_effects=True),
        name="step",
    )(partial, positions, momenta, labels)

    partial = forces(firsts, seconds, count, rows, cols)
    force = pl.pallas_call(
        functools.partial(last_kernel, axes[:1], tiles),
        out_shape=own_shape,
        in_specs=[anywhere, vmem],
        out_specs=vmem,
        scratch_shapes=[
            pltpu.VMEM(row_shape.shape, f32), DMA((col_count - 1,)), DMA((col_count - 1,)), DMA((1,)),
        ],
        compiler_params=pltpu.CompilerParams(collective_id=2, has_side_effects=True),
        name="last",
    )(partial, labels)
    return tuple(
        pl.pallas_call(
            finish_kernel, out_shape=(own_shape,) * 3, in_specs=[vmem] * 3, out_specs=(vmem,) * 3, name="finish"
        )(moved, half, force)
    )


def solution(mesh):
    in_specs = (
        P(None, ("row", "col")),
        P(None, ("row", "col")),
        P(("row", "col")),
        P("row", "col", None),
        P("row", "col", None),
        P("row", "col"),
    )
    out_specs = (P(None, ("row", "col")), P(None, ("row", "col")), P(None, ("row", "col")))
    body = functools.partial(per_device, mesh.shape["row"], mesh.shape["col"])
    return jax.shard_map(body, mesh=mesh, in_specs=in_specs, out_specs=out_specs, check_vma=False)
```

```python
import functools
import math

import jax
import jax.numpy as jnp
from jax import lax
from jax.experimental import pallas as pl
from jax.experimental.pallas import tpu as pltpu
from jax.sharding import PartitionSpec as P

SOFTENING = 0.25
GRAVITY = 0.5
LIGHT_CHARGE = 1.0
HEAVY_CHARGE = 2.5
HALF_STEP = 0.1
TIME_STEP = 0.2
tile_width = 128
unroll = 32
scale = 1.0 / math.log(2.0)
middle = 2.0
depth = 32
MESH = pl.DeviceIdType.MESH


def group_of(axes):
    return 2 * lax.axis_index("row") // axes["row"]


def across(axes):
    return axes["row"] - 1 - lax.axis_index("row")


def column_peers(axes):
    me, size = lax.axis_index("col"), axes["col"]
    return [{"col": lax.rem(me + step, size)} for step in range(1, size)]


def cross_peers(axes):
    me, size = lax.axis_index("col"), axes["col"]
    return [{"row": across(axes), "col": lax.rem(me + step, size)} for step in range(size)]


def row_peers(axes):
    me, size = lax.axis_index("row"), axes["row"]
    return [{"row": lax.rem(me + step, size)} for step in range(1, size)]


def greet(everyone):
    barrier = pltpu.get_barrier_semaphore()
    for peer in everyone:
        pl.semaphore_signal(barrier, inc=1, device_id=peer, device_id_type=MESH)
    pl.semaphore_wait(barrier, len(everyone))


def remote(source, target, sems, which, peer):
    return pltpu.make_async_remote_copy(
        src_ref=source,
        dst_ref=target,
        send_sem=sems[0].at[which],
        recv_sem=sems[1].at[which],
        device_id=peer,
        device_id_type=MESH,
    )


def charge_of(species):
    return jnp.where(species == 1, HEAVY_CHARGE, LIGHT_CHARGE).astype(jnp.float32)


def spread(axes, packed, rows_ref, cols_ref, sems, own_sem, extra=()):
    mine = rows_ref.at[group_of(axes) * axes["col"] + lax.axis_index("col")]
    level = cols_ref.at[lax.axis_index("row")]
    jobs = [(packed, mine, peer) for peer in cross_peers(axes) + column_peers(axes)]
    jobs += [(packed, level, peer) for peer in row_peers(axes)]
    jobs += list(extra)
    copies = [remote(source, target, sems, which, peer) for which, (source, target, peer) in enumerate(jobs)]
    kept = [
        pltpu.make_async_copy(packed, mine, own_sem.at[0]),
        pltpu.make_async_copy(packed, level, own_sem.at[1]),
    ]
    for copy in copies + kept:
        copy.start()
    for copy in kept + copies:
        copy.wait()


def pack(packed, places, charge, tiles):
    for tile in range(tiles):
        lanes = slice(tile * tile_width, (tile + 1) * tile_width)
        packed[4 * tile : 4 * tile + 3, :] = places[:, lanes]
        packed[4 * tile + 3 : 4 * tile + 4, :] = charge[:, lanes]


def gather_kernel(
    axes, tiles, pos_ref, spec_ref, first_ref, second_ref, count_ref, rows_ref, cols_ref, lists_ref,
    packed, listed, send_sem, recv_sem, own_sem,
):
    greet(column_peers(axes) + cross_peers(axes) + row_peers(axes))
    pack(packed, pos_ref[...], charge_of(spec_ref[...]), tiles)
    listed[...] = jnp.zeros_like(listed)
    listed[0:1, :] = first_ref[...]
    listed[1:2, :] = second_ref[...]
    listed[2:3, :] = jnp.broadcast_to(count_ref[...], first_ref.shape)
    target = lists_ref.at[group_of(axes)]
    kept = pltpu.make_async_copy(listed, target, own_sem.at[2])
    kept.start()
    extra = [(listed, target, {"row": across(axes)})]
    spread(axes, packed, rows_ref, cols_ref, (send_sem, recv_sem), own_sem, extra)
    kept.wait()


def collect(axes, partial, arrived, sems, own_sem):
    size, me, group = axes["col"], lax.axis_index("col"), group_of(axes)
    mine = arrived.at[group * size + me]
    jobs = [
        (partial.at[(1 - group) * size + peer["col"]], mine, peer) for peer in cross_peers(axes)
    ]
    jobs += [(partial.at[group * size + peer["col"]], mine, peer) for peer in column_peers(axes)]
    copies = [remote(source, target, sems, which, peer) for which, (source, target, peer) in enumerate(jobs)]
    copies.append(pltpu.make_async_copy(partial.at[group * size + me], mine, own_sem))
    for copy in copies:
        copy.start()
    for copy in copies:
        copy.wait()
    total = arrived[0]
    for index in range(1, 2 * size):
        total = total + arrived[index]
    return total


def unpacked(total, charge, tiles):
    force = jnp.concatenate([total[4 * tile : 4 * tile + 3, :] for tile in range(tiles)], axis=1)
    third = lax.broadcasted_iota(jnp.int32, force.shape, 0) == 2
    return force + jnp.where(third, -GRAVITY * charge, 0.0)


def step_kernel(
    axes, tiles, part_ref, pos_ref, mom_ref, spec_ref, rows_ref, cols_ref, moved_ref, half_ref,
    arrived, packed, send_a, recv_a, send_b, recv_b, own_sem,
):
    greet(column_peers(axes) + cross_peers(axes) + row_peers(axes))
    charge = charge_of(spec_ref[...])
    total = collect(axes, part_ref, arrived, (send_a, recv_a), own_sem.at[0])
    force = unpacked(total, charge, tiles)
    half = mom_ref[...] + HALF_STEP * force
    moved = pos_ref[...] + TIME_STEP * half / charge
    half_ref[...] = half
    moved_ref[...] = moved
    pack(packed, moved, charge, tiles)
    spread(axes, packed, rows_ref, cols_ref, (send_b, recv_b), own_sem.at[pl.ds(1, 2)])


def last_kernel(axes, tiles, part_ref, spec_ref, force_ref, arrived, send_a, recv_a, own_sem):
    greet(column_peers(axes) + cross_peers(axes))
    charge = charge_of(spec_ref[...])
    total = collect(axes, part_ref, arrived, (send_a, recv_a), own_sem.at[0])
    force_ref[...] = unpacked(total, charge, tiles)


def finish_kernel(moved_ref, half_ref, force_ref, trial_ref, ahead_ref, end_ref):
    trial_ref[...] = moved_ref[...]
    ahead_ref[...] = half_ref[...] + HALF_STEP * force_ref[...]
    end_ref[...] = force_ref[...]


def pieces(value):
    high = value.astype(jnp.bfloat16).astype(jnp.float32)
    rest = value - high
    mid = rest.astype(jnp.bfloat16).astype(jnp.float32)
    return high, mid, (rest - mid).astype(jnp.bfloat16).astype(jnp.float32)


pairs_of_pieces = ((0, 0), (0, 1), (1, 0), (0, 2), (2, 0), (1, 1))


def force_kernel(
    axes, tiles, lists_ref, rows_hbm, cols_hbm, out_hbm,
    out_ref, rows_ref, cols_ref, near_f, near, far_f, far, load_f, load, total, sems,
):
    fetches = [
        pltpu.make_async_copy(rows_hbm, rows_ref, sems.at[0]),
        pltpu.make_async_copy(cols_hbm, cols_ref, sems.at[1]),
    ]
    for fetch in fetches:
        fetch.start()
    near_f[...] = jnp.zeros_like(near_f)
    far_f[...] = jnp.zeros_like(far_f)
    load_f[...] = jnp.zeros_like(load_f)
    total[...] = jnp.zeros_like(total)
    for fetch in fetches:
        fetch.wait()

    def component(ref, owner, index):
        return ref[owner, pl.ds(index, tiles, stride=4), :]

    for owner in range(rows_ref.shape[0]):
        here = pl.ds(owner * tiles, tiles)
        square = 0.0
        for axis in range(3):
            value = (component(rows_ref, owner, axis) - middle) * scale
            square = square + value * value
            split = pieces(value)
            for row, (left, _) in enumerate(pairs_of_pieces):
                near_f[here, 6 * axis + row, :] = -2.0 * split[left]
        for row, piece in enumerate(pieces(square)):
            near_f[here, 18 + row, :] = piece
            near_f[here, 21 + row, :] = jnp.ones_like(piece)
    near[...] = near_f[...].astype(jnp.bfloat16)

    for owner in range(cols_ref.shape[0]):
        here = pl.ds(owner * tiles, tiles)
        charge = component(cols_ref, owner, 3)
        square = SOFTENING * scale * scale
        for axis in range(3):
            value = (component(cols_ref, owner, axis) - middle) * scale
            square = square + value * value
            split = pieces(value)
            for row, (_, right) in enumerate(pairs_of_pieces):
                far_f[here, 6 * axis + row, :] = split[right]
            for row, piece in enumerate(pieces(charge * value)):
                load_f[here, 4 * row + axis, :] = piece
        load_f[here, 3, :] = charge
        for row, piece in enumerate(pieces(square)):
            far_f[here, 18 + row, :] = jnp.ones_like(piece)
            far_f[here, 21 + row, :] = piece
    for tile in range(cols_ref.shape[0] * tiles):
        far[tile] = far_f[tile].T.astype(jnp.bfloat16)
    single = load_f[...].astype(jnp.bfloat16)
    load[:, :, :tile_width] = single
    load[:, :, tile_width:] = single

    slots = lists_ref.shape[2]
    group = group_of(axes)
    lower = lists_ref[0, 2, 0]
    count = lower + lists_ref[1, 2, 0]
    middle_slot = (count + 1) // 2
    begin = group * middle_slot
    end = jnp.where(group == 0, middle_slot, count)

    def visit(step, carry):
        start = begin + step * unroll
        firsts, seconds = [], []
        for index in range(unroll):
            slot = jnp.minimum(start + index, count - 1)
            side = (slot >= lower).astype(jnp.int32)
            slot = slot - side * lower
            firsts.append(lists_ref[side, 0, slot] + side * (near.shape[0] // 2))
            seconds.append(lists_ref[side, 1, slot])
        terms = []
        for index in range(unroll):
            square = jnp.dot(far[seconds[index]], near[firsts[index]], preferred_element_type=jnp.float32)
            square = jnp.maximum(square, SOFTENING * scale * scale)
            inverse = lax.rsqrt(square)
            decay = jnp.exp2(-(square * inverse))
            weight = decay * (inverse * inverse) * (inverse + 1.0 / scale)
            high = weight.astype(jnp.bfloat16)
            low = (weight - high.astype(jnp.float32)).astype(jnp.bfloat16)
            both = jnp.concatenate([high, low], axis=0)
            term = jnp.dot(load[seconds[index]], both, preferred_element_type=jnp.float32)
            terms.append(jnp.where(start + index < end, term, 0.0))
        for index in range(unroll):
            total[firsts[index]] += terms[index]
        return carry

    lax.fori_loop(0, (end - begin + unroll - 1) // unroll, visit, 0)

    for owner in range(rows_ref.shape[0]):
        here = pl.ds(owner * tiles, tiles)
        charge = component(rows_ref, owner, 3) * (scale * scale)
        weights = total[here, 3, :]
        for axis in range(3):
            value = (component(rows_ref, owner, axis) - middle) * scale
            moment = total[here, axis, :] + total[here, 4 + axis, :] + total[here, 8 + axis, :]
            out_ref[owner, pl.ds(axis, tiles, stride=4), :] = charge * (value * weights - moment)
        out_ref[owner, pl.ds(3, tiles, stride=4), :] = jnp.zeros_like(charge)
    pltpu.sync_copy(out_ref, out_hbm)


def per_device(row_count, col_count, positions, momenta, species, tile_a, tile_b, tile_count):
    own = positions.shape[1]
    tiles = own // tile_width
    f32 = jnp.float32
    axes = {"col": col_count, "row": row_count}
    across_all = 2 * col_count - 1
    others = across_all + row_count - 1
    vmem = pl.BlockSpec(memory_space=pltpu.VMEM)
    anywhere = pl.BlockSpec(memory_space=pltpu.HBM)
    smem = pl.BlockSpec(memory_space=pltpu.SMEM)
    labels = species.reshape(1, own)
    slots = tile_a.shape[-1]
    firsts = tile_a.reshape(1, slots)
    seconds = tile_b.reshape(1, slots)
    row_shape = jax.ShapeDtypeStruct((2 * col_count, 4 * tiles, tile_width), f32)
    col_shape = jax.ShapeDtypeStruct((row_count, 4 * tiles, tile_width), f32)
    own_shape = jax.ShapeDtypeStruct((3, own), f32)
    DMA = pltpu.SemaphoreType.DMA

    list_shape = jax.ShapeDtypeStruct((2, 8, slots), jnp.int32)
    rows, cols, lists = pl.pallas_call(
        functools.partial(gather_kernel, axes, tiles),
        out_shape=(row_shape, col_shape, list_shape),
        in_specs=[vmem] * 5,
        out_specs=(anywhere,) * 3,
        scratch_shapes=[
            pltpu.VMEM((4 * tiles, tile_width), f32),
            pltpu.VMEM((8, slots), jnp.int32),
            DMA((others + 1,)),
            DMA((others + 1,)),
            DMA((3,)),
        ],
        compiler_params=pltpu.CompilerParams(collective_id=0, has_side_effects=True),
        name="gather",
    )(positions, labels, firsts, seconds, tile_count)

    near_count, far_count = 2 * col_count * tiles, row_count * tiles
    bf16 = jnp.bfloat16
    forces = pl.pallas_call(
        functools.partial(force_kernel, axes, tiles),
        out_shape=row_shape,
        in_specs=[smem] + [anywhere] * 2,
        out_specs=anywhere,
        scratch_shapes=[
            pltpu.VMEM(row_shape.shape, f32),
            pltpu.VMEM(row_shape.shape, f32),
            pltpu.VMEM(col_shape.shape, f32),
            pltpu.VMEM((near_count, depth, tile_width), f32),
            pltpu.VMEM((near_count, depth, tile_width), bf16),
            pltpu.VMEM((far_count, depth, tile_width), f32),
            pltpu.VMEM((far_count, tile_width, depth), bf16),
            pltpu.VMEM((far_count, 16, tile_width), f32),
            pltpu.VMEM((far_count, 16, 2 * tile_width), bf16),
            pltpu.VMEM((near_count, 16, tile_width), f32),
            DMA((2,)),
        ],
        name="forces",
    )

    partial = forces(lists, rows, cols)
    rows, cols, moved, half = pl.pallas_call(
        functools.partial(step_kernel, axes, tiles),
        out_shape=(row_shape, col_shape, own_shape, own_shape),
        in_specs=[anywhere] + [vmem] * 3,
        out_specs=(anywhere, anywhere, vmem, vmem),
        scratch_shapes=[
            pltpu.VMEM(row_shape.shape, f32),
            pltpu.VMEM((4 * tiles, tile_width), f32),
            DMA((across_all,)),
            DMA((across_all,)),
            DMA((others,)),
            DMA((others,)),
            DMA((3,)),
        ],
        compiler_params=pltpu.CompilerParams(collective_id=1, has_side_effects=True),
        name="step",
    )(partial, positions, momenta, labels)

    partial = forces(lists, rows, cols)
    force = pl.pallas_call(
        functools.partial(last_kernel, axes, tiles),
        out_shape=own_shape,
        in_specs=[anywhere, vmem],
        out_specs=vmem,
        scratch_shapes=[
            pltpu.VMEM(row_shape.shape, f32), DMA((across_all,)), DMA((across_all,)), DMA((1,)),
        ],
        compiler_params=pltpu.CompilerParams(collective_id=2, has_side_effects=True),
        name="last",
    )(partial, labels)
    return tuple(
        pl.pallas_call(
            finish_kernel, out_shape=(own_shape,) * 3, in_specs=[vmem] * 3, out_specs=(vmem,) * 3, name="finish"
        )(moved, half, force)
    )


def solution(mesh):
    in_specs = (
        P(None, ("row", "col")),
        P(None, ("row", "col")),
        P(("row", "col")),
        P("row", "col", None),
        P("row", "col", None),
        P("row", "col"),
    )
    out_specs = (P(None, ("row", "col")), P(None, ("row", "col")), P(None, ("row", "col")))
    body = functools.partial(per_device, mesh.shape["row"], mesh.shape["col"])
    return jax.shard_map(body, mesh=mesh, in_specs=in_specs, out_specs=out_specs, check_vma=False)
```

```python
import functools
import math

import jax
import jax.numpy as jnp
from jax import lax
from jax.experimental import pallas as pl
from jax.experimental.pallas import tpu as pltpu
from jax.sharding import PartitionSpec as P

SOFTENING = 0.25
GRAVITY = 0.5
LIGHT_CHARGE = 1.0
HEAVY_CHARGE = 2.5
HALF_STEP = 0.1
TIME_STEP = 0.2
tile_width = 128
unroll = 48
scale = 1.0 / math.log(2.0)
middle = 2.0
depth = 32
MESH = pl.DeviceIdType.MESH


def group_of(axes):
    return 2 * lax.axis_index("row") // axes["row"]


def across(axes):
    return axes["row"] - 1 - lax.axis_index("row")


def column_peers(axes):
    me, size = lax.axis_index("col"), axes["col"]
    return [{"col": lax.rem(me + step, size)} for step in range(1, size)]


def cross_peers(axes):
    me, size = lax.axis_index("col"), axes["col"]
    return [{"row": across(axes), "col": lax.rem(me + step, size)} for step in range(size)]


def row_peers(axes):
    me, size = lax.axis_index("row"), axes["row"]
    return [{"row": lax.rem(me + step, size)} for step in range(1, size)]


def greet(everyone, meanwhile=lambda: None):
    barrier = pltpu.get_barrier_semaphore()
    for peer in everyone:
        pl.semaphore_signal(barrier, inc=1, device_id=peer, device_id_type=MESH)
    meanwhile()
    pl.semaphore_wait(barrier, len(everyone))


def remote(source, target, sems, which, peer):
    return pltpu.make_async_remote_copy(
        src_ref=source,
        dst_ref=target,
        send_sem=sems[0].at[which],
        recv_sem=sems[1].at[which],
        device_id=peer,
        device_id_type=MESH,
    )


def charge_of(species):
    return jnp.where(species == 1, HEAVY_CHARGE, LIGHT_CHARGE).astype(jnp.float32)


def spread(axes, packed, rows_ref, cols_ref, sems, own_sem, extra=()):
    mine = rows_ref.at[group_of(axes) * axes["col"] + lax.axis_index("col")]
    level = cols_ref.at[lax.axis_index("row")]
    jobs = [(packed, mine, peer) for peer in cross_peers(axes) + column_peers(axes)]
    jobs += [(packed, level, peer) for peer in row_peers(axes)]
    jobs += list(extra)
    copies = [remote(source, target, sems, which, peer) for which, (source, target, peer) in enumerate(jobs)]
    kept = [
        pltpu.make_async_copy(packed, mine, own_sem.at[0]),
        pltpu.make_async_copy(packed, level, own_sem.at[1]),
    ]
    for copy in copies + kept:
        copy.start()
    for copy in kept + copies:
        copy.wait()


def pack(packed, places, charge, tiles):
    for tile in range(tiles):
        lanes = slice(tile * tile_width, (tile + 1) * tile_width)
        packed[4 * tile : 4 * tile + 3, :] = places[:, lanes]
        packed[4 * tile + 3 : 4 * tile + 4, :] = charge[:, lanes]


def gather_kernel(
    axes, tiles, pos_ref, spec_ref, first_ref, second_ref, count_ref, rows_ref, cols_ref, lists_ref,
    packed, listed, send_sem, recv_sem, own_sem,
):
    def prepare():
        pack(packed, pos_ref[...], charge_of(spec_ref[...]), tiles)
        listed[...] = jnp.zeros_like(listed)
        listed[0:1, :] = first_ref[...]
        listed[1:2, :] = second_ref[...]
        listed[2:3, :] = jnp.broadcast_to(count_ref[...], first_ref.shape)

    greet(column_peers(axes) + cross_peers(axes) + row_peers(axes), prepare)
    target = lists_ref.at[group_of(axes)]
    kept = pltpu.make_async_copy(listed, target, own_sem.at[2])
    kept.start()
    extra = [(listed, target, {"row": across(axes)})]
    spread(axes, packed, rows_ref, cols_ref, (send_sem, recv_sem), own_sem, extra)
    kept.wait()


def collect(axes, partial, arrived, sems, own_sem):
    size, me, group = axes["col"], lax.axis_index("col"), group_of(axes)
    mine = arrived.at[group * size + me]
    jobs = [
        (partial.at[(1 - group) * size + peer["col"]], mine, peer) for peer in cross_peers(axes)
    ]
    jobs += [(partial.at[group * size + peer["col"]], mine, peer) for peer in column_peers(axes)]
    copies = [remote(source, target, sems, which, peer) for which, (source, target, peer) in enumerate(jobs)]
    copies.append(pltpu.make_async_copy(partial.at[group * size + me], mine, own_sem))
    for copy in copies:
        copy.start()
    for copy in copies:
        copy.wait()
    total = arrived[0]
    for index in range(1, 2 * size):
        total = total + arrived[index]
    return total


def unpacked(total, charge, tiles):
    force = jnp.concatenate([total[4 * tile : 4 * tile + 3, :] for tile in range(tiles)], axis=1)
    third = lax.broadcasted_iota(jnp.int32, force.shape, 0) == 2
    return force + jnp.where(third, -GRAVITY * charge, 0.0)


def step_kernel(
    axes, tiles, part_ref, pos_ref, mom_ref, spec_ref, rows_ref, cols_ref, moved_ref, half_ref,
    arrived, packed, send_a, recv_a, send_b, recv_b, own_sem,
):
    greet(column_peers(axes) + cross_peers(axes) + row_peers(axes))
    charge = charge_of(spec_ref[...])
    total = collect(axes, part_ref, arrived, (send_a, recv_a), own_sem.at[0])
    force = unpacked(total, charge, tiles)
    half = mom_ref[...] + HALF_STEP * force
    moved = pos_ref[...] + TIME_STEP * half / charge
    half_ref[...] = half
    moved_ref[...] = moved
    pack(packed, moved, charge, tiles)
    spread(axes, packed, rows_ref, cols_ref, (send_b, recv_b), own_sem.at[pl.ds(1, 2)])


def last_kernel(axes, tiles, part_ref, spec_ref, force_ref, arrived, send_a, recv_a, own_sem):
    greet(column_peers(axes) + cross_peers(axes))
    charge = charge_of(spec_ref[...])
    total = collect(axes, part_ref, arrived, (send_a, recv_a), own_sem.at[0])
    force_ref[...] = unpacked(total, charge, tiles)


def finish_kernel(moved_ref, half_ref, force_ref, trial_ref, ahead_ref, end_ref):
    trial_ref[...] = moved_ref[...]
    ahead_ref[...] = half_ref[...] + HALF_STEP * force_ref[...]
    end_ref[...] = force_ref[...]


def pieces(value):
    high = value.astype(jnp.bfloat16).astype(jnp.float32)
    rest = value - high
    mid = rest.astype(jnp.bfloat16).astype(jnp.float32)
    return high, mid, (rest - mid).astype(jnp.bfloat16).astype(jnp.float32)


pairs_of_pieces = ((0, 0), (0, 1), (1, 0), (0, 2), (2, 0), (1, 1))


def force_kernel(
    axes, tiles, lists_ref, rows_hbm, cols_hbm, out_hbm,
    out_ref, rows_ref, cols_ref, near_f, near, far_f, far, load_f, load, total, sems,
):
    fetches = [
        pltpu.make_async_copy(rows_hbm, rows_ref, sems.at[0]),
        pltpu.make_async_copy(cols_hbm, cols_ref, sems.at[1]),
    ]
    for fetch in fetches:
        fetch.start()
    near_f[...] = jnp.zeros_like(near_f)
    far_f[...] = jnp.zeros_like(far_f)
    load_f[...] = jnp.zeros_like(load_f)
    total[...] = jnp.zeros_like(total)
    for fetch in fetches:
        fetch.wait()

    def component(ref, owner, index):
        return ref[owner, pl.ds(index, tiles, stride=4), :]

    for owner in range(rows_ref.shape[0]):
        here = pl.ds(owner * tiles, tiles)
        square = 0.0
        for axis in range(3):
            value = (component(rows_ref, owner, axis) - middle) * scale
            square = square + value * value
            split = pieces(value)
            for row, (left, _) in enumerate(pairs_of_pieces):
                near_f[here, 6 * axis + row, :] = -2.0 * split[left]
        for row, piece in enumerate(pieces(square)):
            near_f[here, 18 + row, :] = piece
            near_f[here, 21 + row, :] = jnp.ones_like(piece)
    near[...] = near_f[...].astype(jnp.bfloat16)

    for owner in range(cols_ref.shape[0]):
        here = pl.ds(owner * tiles, tiles)
        charge = component(cols_ref, owner, 3)
        square = SOFTENING * scale * scale
        for axis in range(3):
            value = (component(cols_ref, owner, axis) - middle) * scale
            square = square + value * value
            split = pieces(value)
            for row, (_, right) in enumerate(pairs_of_pieces):
                far_f[here, 6 * axis + row, :] = split[right]
            for row, piece in enumerate(pieces(charge * value)):
                load_f[here, 4 * row + axis, :] = piece
        load_f[here, 3, :] = charge
        for row, piece in enumerate(pieces(square)):
            far_f[here, 18 + row, :] = jnp.ones_like(piece)
            far_f[here, 21 + row, :] = piece
    for tile in range(cols_ref.shape[0] * tiles):
        far[tile] = far_f[tile].T.astype(jnp.bfloat16)
    single = load_f[...].astype(jnp.bfloat16)
    load[:, :, :tile_width] = single
    load[:, :, tile_width:] = single

    slots = lists_ref.shape[2]
    group = group_of(axes)
    lower = lists_ref[0, 2, 0]
    count = lower + lists_ref[1, 2, 0]
    middle_slot = (count + 1) // 2
    begin = group * middle_slot
    end = jnp.where(group == 0, middle_slot, count)

    def visit(step, carry):
        start = begin + step * unroll
        firsts, seconds = [], []
        for index in range(unroll):
            slot = jnp.minimum(start + index, count - 1)
            side = (slot >= lower).astype(jnp.int32)
            slot = slot - side * lower
            firsts.append(lists_ref[side, 0, slot] + side * (near.shape[0] // 2))
            seconds.append(lists_ref[side, 1, slot])
        terms = []
        for index in range(unroll):
            square = jnp.dot(far[seconds[index]], near[firsts[index]], preferred_element_type=jnp.float32)
            square = jnp.maximum(square, SOFTENING * scale * scale)
            inverse = lax.rsqrt(square)
            decay = jnp.exp2(-(square * inverse))
            weight = decay * (inverse * inverse) * (inverse + 1.0 / scale)
            high = weight.astype(jnp.bfloat16)
            low = (weight - high.astype(jnp.float32)).astype(jnp.bfloat16)
            both = jnp.concatenate([high, low], axis=0)
            term = jnp.dot(load[seconds[index]], both, preferred_element_type=jnp.float32)
            terms.append(jnp.where(start + index < end, term, 0.0))
        for index in range(unroll):
            total[firsts[index]] += terms[index]
        return carry

    lax.fori_loop(0, (end - begin + unroll - 1) // unroll, visit, 0)

    for owner in range(rows_ref.shape[0]):
        here = pl.ds(owner * tiles, tiles)
        charge = component(rows_ref, owner, 3) * (scale * scale)
        weights = total[here, 3, :]
        for axis in range(3):
            value = (component(rows_ref, owner, axis) - middle) * scale
            moment = total[here, axis, :] + total[here, 4 + axis, :] + total[here, 8 + axis, :]
            out_ref[owner, pl.ds(axis, tiles, stride=4), :] = charge * (value * weights - moment)
        out_ref[owner, pl.ds(3, tiles, stride=4), :] = jnp.zeros_like(charge)
    pltpu.sync_copy(out_ref, out_hbm)


def per_device(row_count, col_count, positions, momenta, species, tile_a, tile_b, tile_count):
    own = positions.shape[1]
    tiles = own // tile_width
    f32 = jnp.float32
    axes = {"col": col_count, "row": row_count}
    across_all = 2 * col_count - 1
    others = across_all + row_count - 1
    vmem = pl.BlockSpec(memory_space=pltpu.VMEM)
    anywhere = pl.BlockSpec(memory_space=pltpu.HBM)
    smem = pl.BlockSpec(memory_space=pltpu.SMEM)
    labels = species.reshape(1, own)
    slots = tile_a.shape[-1]
    firsts = tile_a.reshape(1, slots)
    seconds = tile_b.reshape(1, slots)
    row_shape = jax.ShapeDtypeStruct((2 * col_count, 4 * tiles, tile_width), f32)
    col_shape = jax.ShapeDtypeStruct((row_count, 4 * tiles, tile_width), f32)
    own_shape = jax.ShapeDtypeStruct((3, own), f32)
    DMA = pltpu.SemaphoreType.DMA

    list_shape = jax.ShapeDtypeStruct((2, 8, slots), jnp.int32)
    rows, cols, lists = pl.pallas_call(
        functools.partial(gather_kernel, axes, tiles),
        out_shape=(row_shape, col_shape, list_shape),
        in_specs=[vmem] * 5,
        out_specs=(anywhere,) * 3,
        scratch_shapes=[
            pltpu.VMEM((4 * tiles, tile_width), f32),
            pltpu.VMEM((8, slots), jnp.int32),
            DMA((others + 1,)),
            DMA((others + 1,)),
            DMA((3,)),
        ],
        compiler_params=pltpu.CompilerParams(collective_id=0, has_side_effects=True),
        name="gather",
    )(positions, labels, firsts, seconds, tile_count)

    near_count, far_count = 2 * col_count * tiles, row_count * tiles
    bf16 = jnp.bfloat16
    forces = pl.pallas_call(
        functools.partial(force_kernel, axes, tiles),
        out_shape=row_shape,
        in_specs=[smem] + [anywhere] * 2,
        out_specs=anywhere,
        scratch_shapes=[
            pltpu.VMEM(row_shape.shape, f32),
            pltpu.VMEM(row_shape.shape, f32),
            pltpu.VMEM(col_shape.shape, f32),
            pltpu.VMEM((near_count, depth, tile_width), f32),
            pltpu.VMEM((near_count, depth, tile_width), bf16),
            pltpu.VMEM((far_count, depth, tile_width), f32),
            pltpu.VMEM((far_count, tile_width, depth), bf16),
            pltpu.VMEM((far_count, 16, tile_width), f32),
            pltpu.VMEM((far_count, 16, 2 * tile_width), bf16),
            pltpu.VMEM((near_count, 16, tile_width), f32),
            DMA((2,)),
        ],
        name="forces",
    )

    partial = forces(lists, rows, cols)
    rows, cols, moved, half = pl.pallas_call(
        functools.partial(step_kernel, axes, tiles),
        out_shape=(row_shape, col_shape, own_shape, own_shape),
        in_specs=[anywhere] + [vmem] * 3,
        out_specs=(anywhere, anywhere, vmem, vmem),
        scratch_shapes=[
            pltpu.VMEM(row_shape.shape, f32),
            pltpu.VMEM((4 * tiles, tile_width), f32),
            DMA((across_all,)),
            DMA((across_all,)),
            DMA((others,)),
            DMA((others,)),
            DMA((3,)),
        ],
        compiler_params=pltpu.CompilerParams(collective_id=1, has_side_effects=True),
        name="step",
    )(partial, positions, momenta, labels)

    partial = forces(lists, rows, cols)
    force = pl.pallas_call(
        functools.partial(last_kernel, axes, tiles),
        out_shape=own_shape,
        in_specs=[anywhere, vmem],
        out_specs=vmem,
        scratch_shapes=[
            pltpu.VMEM(row_shape.shape, f32), DMA((across_all,)), DMA((across_all,)), DMA((1,)),
        ],
        compiler_params=pltpu.CompilerParams(collective_id=2, has_side_effects=True),
        name="last",
    )(partial, labels)
    return tuple(
        pl.pallas_call(
            finish_kernel, out_shape=(own_shape,) * 3, in_specs=[vmem] * 3, out_specs=(vmem,) * 3, name="finish"
        )(moved, half, force)
    )


def solution(mesh):
    in_specs = (
        P(None, ("row", "col")),
        P(None, ("row", "col")),
        P(("row", "col")),
        P("row", "col", None),
        P("row", "col", None),
        P("row", "col"),
    )
    out_specs = (P(None, ("row", "col")), P(None, ("row", "col")), P(None, ("row", "col")))
    body = functools.partial(per_device, mesh.shape["row"], mesh.shape["col"])
    return jax.shard_map(body, mesh=mesh, in_specs=in_specs, out_specs=out_specs, check_vma=False)
```

```python
import functools
import math

import jax
import jax.numpy as jnp
from jax import lax
from jax.experimental import pallas as pl
from jax.experimental.pallas import tpu as pltpu
from jax.sharding import PartitionSpec as P

SOFTENING = 0.25
GRAVITY = 0.5
LIGHT_CHARGE = 1.0
HEAVY_CHARGE = 2.5
HALF_STEP = 0.1
TIME_STEP = 0.2
tile_width = 128
unroll = 48
scale = 1.0 / math.log(2.0)
middle = 2.0
depth = 32
MESH = pl.DeviceIdType.MESH


def group_of(axes):
    return 2 * lax.axis_index("row") // axes["row"]


def across(axes):
    return axes["row"] - 1 - lax.axis_index("row")


def column_peers(axes):
    me, size = lax.axis_index("col"), axes["col"]
    return [{"col": lax.rem(me + step, size)} for step in range(1, size)]


def cross_peers(axes):
    me, size = lax.axis_index("col"), axes["col"]
    return [{"row": across(axes), "col": lax.rem(me + step, size)} for step in range(size)]


def row_peers(axes):
    me, size = lax.axis_index("row"), axes["row"]
    return [{"row": lax.rem(me + step, size)} for step in range(1, size)]


def greet(everyone, meanwhile=lambda: None):
    barrier = pltpu.get_barrier_semaphore()
    for peer in everyone:
        pl.semaphore_signal(barrier, inc=1, device_id=peer, device_id_type=MESH)
    meanwhile()
    pl.semaphore_wait(barrier, len(everyone))


def remote(source, target, sems, which, peer):
    return pltpu.make_async_remote_copy(
        src_ref=source,
        dst_ref=target,
        send_sem=sems[0].at[which],
        recv_sem=sems[1].at[which],
        device_id=peer,
        device_id_type=MESH,
    )


def charge_of(species):
    return jnp.where(species == 1, HEAVY_CHARGE, LIGHT_CHARGE).astype(jnp.float32)


def spread(axes, packed, rows_ref, cols_ref, sems, own_sem, extra=()):
    mine = rows_ref.at[group_of(axes) * axes["col"] + lax.axis_index("col")]
    level = cols_ref.at[lax.axis_index("row")]
    jobs = [(packed, mine, peer) for peer in cross_peers(axes) + column_peers(axes)]
    jobs += [(packed, level, peer) for peer in row_peers(axes)]
    jobs += list(extra)
    copies = [remote(source, target, sems, which, peer) for which, (source, target, peer) in enumerate(jobs)]
    kept = [
        pltpu.make_async_copy(packed, mine, own_sem.at[0]),
        pltpu.make_async_copy(packed, level, own_sem.at[1]),
    ]
    for copy in copies + kept:
        copy.start()
    for copy in kept + copies:
        copy.wait()


def pack(packed, places, charge, tiles):
    for tile in range(tiles):
        lanes = slice(tile * tile_width, (tile + 1) * tile_width)
        packed[4 * tile : 4 * tile + 3, :] = places[:, lanes]
        packed[4 * tile + 3 : 4 * tile + 4, :] = charge[:, lanes]


def gather_kernel(
    axes, tiles, pos_ref, spec_ref, first_ref, second_ref, count_ref, rows_ref, cols_ref, lists_ref,
    packed, listed, send_sem, recv_sem, own_sem,
):
    def prepare():
        pack(packed, pos_ref[...], charge_of(spec_ref[...]), tiles)
        listed[...] = jnp.zeros_like(listed)
        listed[0:1, :] = first_ref[...]
        listed[1:2, :] = second_ref[...]
        listed[2:3, :] = jnp.broadcast_to(count_ref[...], first_ref.shape)

    greet(column_peers(axes) + cross_peers(axes) + row_peers(axes), prepare)
    target = lists_ref.at[group_of(axes)]
    kept = pltpu.make_async_copy(listed, target, own_sem.at[2])
    kept.start()
    extra = [(listed, target, {"row": across(axes)})]
    spread(axes, packed, rows_ref, cols_ref, (send_sem, recv_sem), own_sem, extra)
    kept.wait()


def collect(axes, partial, arrived, sems, own_sem):
    size, me, group = axes["col"], lax.axis_index("col"), group_of(axes)
    mine = arrived.at[group * size + me]
    jobs = [
        (partial.at[(1 - group) * size + peer["col"]], mine, peer) for peer in cross_peers(axes)
    ]
    jobs += [(partial.at[group * size + peer["col"]], mine, peer) for peer in column_peers(axes)]
    copies = [remote(source, target, sems, which, peer) for which, (source, target, peer) in enumerate(jobs)]
    copies.append(pltpu.make_async_copy(partial.at[group * size + me], mine, own_sem))
    for copy in copies:
        copy.start()
    for copy in copies:
        copy.wait()
    total = arrived[0]
    for index in range(1, 2 * size):
        total = total + arrived[index]
    return total


def unpacked(total, charge, tiles):
    force = jnp.concatenate([total[4 * tile : 4 * tile + 3, :] for tile in range(tiles)], axis=1)
    third = lax.broadcasted_iota(jnp.int32, force.shape, 0) == 2
    return force + jnp.where(third, -GRAVITY * charge, 0.0)


def step_kernel(
    axes, tiles, part_ref, pos_ref, mom_ref, spec_ref, rows_ref, cols_ref, moved_ref, half_ref,
    arrived, packed, send_a, recv_a, send_b, recv_b, own_sem,
):
    greet(column_peers(axes) + cross_peers(axes) + row_peers(axes))
    charge = charge_of(spec_ref[...])
    total = collect(axes, part_ref, arrived, (send_a, recv_a), own_sem.at[0])
    force = unpacked(total, charge, tiles)
    half = mom_ref[...] + HALF_STEP * force
    moved = pos_ref[...] + TIME_STEP * half / charge
    half_ref[...] = half
    moved_ref[...] = moved
    pack(packed, moved, charge, tiles)
    spread(axes, packed, rows_ref, cols_ref, (send_b, recv_b), own_sem.at[pl.ds(1, 2)])


def last_kernel(axes, tiles, part_ref, spec_ref, force_ref, arrived, send_a, recv_a, own_sem):
    greet(column_peers(axes) + cross_peers(axes))
    charge = charge_of(spec_ref[...])
    total = collect(axes, part_ref, arrived, (send_a, recv_a), own_sem.at[0])
    force_ref[...] = unpacked(total, charge, tiles)


def finish_kernel(moved_ref, half_ref, force_ref, trial_ref, ahead_ref, end_ref):
    trial_ref[...] = moved_ref[...]
    ahead_ref[...] = half_ref[...] + HALF_STEP * force_ref[...]
    end_ref[...] = force_ref[...]


def pieces(value):
    high = value.astype(jnp.bfloat16).astype(jnp.float32)
    rest = value - high
    mid = rest.astype(jnp.bfloat16).astype(jnp.float32)
    return high, mid, (rest - mid).astype(jnp.bfloat16).astype(jnp.float32)


pairs_of_pieces = ((0, 0), (0, 1), (1, 0), (0, 2), (2, 0), (1, 1))


def force_kernel(
    axes, tiles, lists_ref, rows_hbm, cols_hbm, out_hbm,
    out_ref, rows_ref, cols_ref, near_f, near, far_f, far, load_f, load, total, sems,
):
    fetches = [
        pltpu.make_async_copy(rows_hbm, rows_ref, sems.at[0]),
        pltpu.make_async_copy(cols_hbm, cols_ref, sems.at[1]),
    ]
    for fetch in fetches:
        fetch.start()
    near_f[...] = jnp.zeros_like(near_f)
    far_f[...] = jnp.zeros_like(far_f)
    load_f[...] = jnp.zeros_like(load_f)
    total[...] = jnp.zeros_like(total)
    for fetch in fetches:
        fetch.wait()

    def flat(ref):
        return ref.reshape(ref.shape[0] * ref.shape[1], ref.shape[2])

    rows_flat, cols_flat, out_flat = flat(rows_ref), flat(cols_ref), flat(out_ref)

    def component(ref, owner, index):
        return ref[pl.ds(4 * owner * batch + index, batch, stride=4), :]

    batch = 2 * tiles
    for owner in range(rows_ref.shape[0] // 2):
        here = pl.ds(owner * batch, batch)
        square = 0.0
        for axis in range(3):
            value = (component(rows_flat, owner, axis) - middle) * scale
            square = square + value * value
            split = pieces(value)
            for row, (left, _) in enumerate(pairs_of_pieces):
                near_f[here, 6 * axis + row, :] = -2.0 * split[left]
        for row, piece in enumerate(pieces(square)):
            near_f[here, 18 + row, :] = piece
            near_f[here, 21 + row, :] = jnp.ones_like(piece)
    near[...] = near_f[...].astype(jnp.bfloat16)

    for owner in range(cols_ref.shape[0] // 2):
        here = pl.ds(owner * batch, batch)
        charge = component(cols_flat, owner, 3)
        square = SOFTENING * scale * scale
        for axis in range(3):
            value = (component(cols_flat, owner, axis) - middle) * scale
            square = square + value * value
            split = pieces(value)
            for row, (_, right) in enumerate(pairs_of_pieces):
                far_f[here, 6 * axis + row, :] = split[right]
            for row, piece in enumerate(pieces(charge * value)):
                load_f[here, 4 * row + axis, :] = piece
        load_f[here, 3, :] = charge
        for row, piece in enumerate(pieces(square)):
            far_f[here, 18 + row, :] = jnp.ones_like(piece)
            far_f[here, 21 + row, :] = piece
    for tile in range(cols_ref.shape[0] * tiles):
        far[tile] = far_f[tile].T.astype(jnp.bfloat16)
    single = load_f[...].astype(jnp.bfloat16)
    load[:, :, :tile_width] = single
    load[:, :, tile_width:] = single

    slots = lists_ref.shape[2]
    group = group_of(axes)
    lower = lists_ref[0, 2, 0]
    count = lower + lists_ref[1, 2, 0]
    middle_slot = (count + 1) // 2
    begin = group * middle_slot
    end = jnp.where(group == 0, middle_slot, count)

    def visit(step, carry):
        start = begin + step * unroll
        firsts, seconds = [], []
        for index in range(unroll):
            slot = jnp.minimum(start + index, count - 1)
            side = (slot >= lower).astype(jnp.int32)
            slot = slot - side * lower
            firsts.append(lists_ref[side, 0, slot] + side * (near.shape[0] // 2))
            seconds.append(lists_ref[side, 1, slot])
        terms = []
        for index in range(unroll):
            square = jnp.dot(far[seconds[index]], near[firsts[index]], preferred_element_type=jnp.float32)
            square = jnp.maximum(square, SOFTENING * scale * scale)
            inverse = lax.rsqrt(square)
            decay = jnp.exp2(-(square * inverse))
            weight = decay * (inverse * inverse) * (inverse + 1.0 / scale)
            high = weight.astype(jnp.bfloat16)
            low = (weight - high.astype(jnp.float32)).astype(jnp.bfloat16)
            both = jnp.concatenate([high, low], axis=0)
            term = jnp.dot(load[seconds[index]], both, preferred_element_type=jnp.float32)
            terms.append(jnp.where(start + index < end, term, 0.0))
        for index in range(unroll):
            total[firsts[index]] += terms[index]
        return carry

    lax.fori_loop(0, (end - begin + unroll - 1) // unroll, visit, 0)

    for owner in range(rows_ref.shape[0] // 2):
        here = pl.ds(owner * batch, batch)
        charge = component(rows_flat, owner, 3) * (scale * scale)
        weights = total[here, 3, :]
        for axis in range(3):
            value = (component(rows_flat, owner, axis) - middle) * scale
            moment = total[here, axis, :] + total[here, 4 + axis, :] + total[here, 8 + axis, :]
            out_flat[pl.ds(4 * owner * batch + axis, batch, stride=4), :] = charge * (value * weights - moment)
        out_flat[pl.ds(4 * owner * batch + 3, batch, stride=4), :] = jnp.zeros_like(charge)
    pltpu.sync_copy(out_ref, out_hbm)


def per_device(row_count, col_count, positions, momenta, species, tile_a, tile_b, tile_count):
    own = positions.shape[1]
    tiles = own // tile_width
    f32 = jnp.float32
    axes = {"col": col_count, "row": row_count}
    across_all = 2 * col_count - 1
    others = across_all + row_count - 1
    vmem = pl.BlockSpec(memory_space=pltpu.VMEM)
    anywhere = pl.BlockSpec(memory_space=pltpu.HBM)
    smem = pl.BlockSpec(memory_space=pltpu.SMEM)
    labels = species.reshape(1, own)
    slots = tile_a.shape[-1]
    firsts = tile_a.reshape(1, slots)
    seconds = tile_b.reshape(1, slots)
    row_shape = jax.ShapeDtypeStruct((2 * col_count, 4 * tiles, tile_width), f32)
    col_shape = jax.ShapeDtypeStruct((row_count, 4 * tiles, tile_width), f32)
    own_shape = jax.ShapeDtypeStruct((3, own), f32)
    DMA = pltpu.SemaphoreType.DMA

    list_shape = jax.ShapeDtypeStruct((2, 8, slots), jnp.int32)
    rows, cols, lists = pl.pallas_call(
        functools.partial(gather_kernel, axes, tiles),
        out_shape=(row_shape, col_shape, list_shape),
        in_specs=[vmem] * 5,
        out_specs=(anywhere,) * 3,
        scratch_shapes=[
            pltpu.VMEM((4 * tiles, tile_width), f32),
            pltpu.VMEM((8, slots), jnp.int32),
            DMA((others + 1,)),
            DMA((others + 1,)),
            DMA((3,)),
        ],
        compiler_params=pltpu.CompilerParams(collective_id=0, has_side_effects=True),
        name="gather",
    )(positions, labels, firsts, seconds, tile_count)

    near_count, far_count = 2 * col_count * tiles, row_count * tiles
    bf16 = jnp.bfloat16
    forces = pl.pallas_call(
        functools.partial(force_kernel, axes, tiles),
        out_shape=row_shape,
        in_specs=[smem] + [anywhere] * 2,
        out_specs=anywhere,
        scratch_shapes=[
            pltpu.VMEM(row_shape.shape, f32),
            pltpu.VMEM(row_shape.shape, f32),
            pltpu.VMEM(col_shape.shape, f32),
            pltpu.VMEM((near_count, depth, tile_width), f32),
            pltpu.VMEM((near_count, depth, tile_width), bf16),
            pltpu.VMEM((far_count, depth, tile_width), f32),
            pltpu.VMEM((far_count, tile_width, depth), bf16),
            pltpu.VMEM((far_count, 16, tile_width), f32),
            pltpu.VMEM((far_count, 16, 2 * tile_width), bf16),
            pltpu.VMEM((near_count, 16, tile_width), f32),
            DMA((2,)),
        ],
        name="forces",
    )

    partial = forces(lists, rows, cols)
    rows, cols, moved, half = pl.pallas_call(
        functools.partial(step_kernel, axes, tiles),
        out_shape=(row_shape, col_shape, own_shape, own_shape),
        in_specs=[anywhere] + [vmem] * 3,
        out_specs=(anywhere, anywhere, vmem, vmem),
        scratch_shapes=[
            pltpu.VMEM(row_shape.shape, f32),
            pltpu.VMEM((4 * tiles, tile_width), f32),
            DMA((across_all,)),
            DMA((across_all,)),
            DMA((others,)),
            DMA((others,)),
            DMA((3,)),
        ],
        compiler_params=pltpu.CompilerParams(collective_id=1, has_side_effects=True),
        name="step",
    )(partial, positions, momenta, labels)

    partial = forces(lists, rows, cols)
    force = pl.pallas_call(
        functools.partial(last_kernel, axes, tiles),
        out_shape=own_shape,
        in_specs=[anywhere, vmem],
        out_specs=vmem,
        scratch_shapes=[
            pltpu.VMEM(row_shape.shape, f32), DMA((across_all,)), DMA((across_all,)), DMA((1,)),
        ],
        compiler_params=pltpu.CompilerParams(collective_id=2, has_side_effects=True),
        name="last",
    )(partial, labels)
    return tuple(
        pl.pallas_call(
            finish_kernel, out_shape=(own_shape,) * 3, in_specs=[vmem] * 3, out_specs=(vmem,) * 3, name="finish"
        )(moved, half, force)
    )


def solution(mesh):
    in_specs = (
        P(None, ("row", "col")),
        P(None, ("row", "col")),
        P(("row", "col")),
        P("row", "col", None),
        P("row", "col", None),
        P("row", "col"),
    )
    out_specs = (P(None, ("row", "col")), P(None, ("row", "col")), P(None, ("row", "col")))
    body = functools.partial(per_device, mesh.shape["row"], mesh.shape["col"])
    return jax.shard_map(body, mesh=mesh, in_specs=in_specs, out_specs=out_specs, check_vma=False)
```
